32 devices in a mesh: dp: 8 (over z, x), tensor: 4 (over y, core).
Axes of the slice: x: 2, y: 2, z: 4, core: 2. Of those that a mesh axis runs over, the one named last changes fastest.
Arguments:
- hidden: bfloat16 [2048, 2048], P('dp'), may hold values from -200 to 200
- norm_gain: float32 [2048], replicated, may hold values from 0.5 to 2
- expert_ids: int32 [2048, 8], P(('dp', 'tensor')), may hold values from 0 to 31, all different within a row; in each aligned block of 64 rows (0 to 63, 64 to 127, ...) at most 32 rows name the same one
- gate_probs: float32 [2048, 8], P(('dp', 'tensor')), may hold values from 0.05 to 0.5
- out_grad: bfloat16 [2048, 2048], P(('dp', 'tensor')), may hold values from -8 to 8
- gate_weight: bfloat16 [32, 2048, 768], P(('dp', 'tensor')), may hold values from -0.125 to 0.125
- up_weight: bfloat16 [32, 2048, 768], P(('dp', 'tensor')), may hold values from -0.125 to 0.125
- down_weight: bfloat16 [32, 768, 2048], P(('dp', 'tensor')), may hold values from -0.21875 to 0.21875
Outputs:
- layer_out: bfloat16 [2048, 2048], P(('dp', 'tensor'))
- input_grad: bfloat16 [2048, 2048], P('dp')
- gate_grad: float32 [2048, 8], P(('dp', 'tensor'))
- gain_grad: float32 [2048], replicated
- gate_weight_grad: bfloat16 [32, 2048, 768], P(('dp', 'tensor'))
- up_weight_grad: bfloat16 [32, 2048, 768], P(('dp', 'tensor'))
- down_weight_grad: bfloat16 [32, 768, 2048], P(('dp', 'tensor'))
The draws below stay inside these ranges and needn't reach their ends.
Inputs may be any that keep to these rules, and one draw needn't show every extreme that they name: `expert_ids`: within the rows of one device no expert is named by more than 32 rows, a bound that some block reaches.
All inputs are finite; a program needn't handle non-finite values.
Results may differ from the reference program's by a relative error of at most 0.0072.
Values may be sent and summed in bfloat16 or wider, within the bound.
A program may use at most 128 MiB of HBM per device.

```python
import math
import jax
import jax.numpy as jnp
import numpy as np
from jax import lax

D = 2048
FF = 768
TOPK = 8
EXPERTS = 32
TOKENS = 2048
ROWS_DEV = 64
CAP = 32
SLOTS = 1024


def draw_hidden(key, part):
    first, second, third = jax.random.split(key, 3)
    row_scale = jnp.exp(jax.random.uniform(first, (TOKENS, 1), jnp.float32, 0.0, math.log(10.0)))
    col_scale = jnp.exp(jax.random.uniform(second, (1, D), jnp.float32, 0.0, math.log(10.0)))
    base = jnp.clip(jax.random.normal(third, (TOKENS, D), jnp.float32), -6.0, 6.0)
    return (0.3 * base * row_scale * col_scale).astype(jnp.bfloat16)


def draw_out_grad(key, part):
    first = jax.random.fold_in(key, 0)
    ramp = jnp.arange(TOKENS, dtype=jnp.float32)[:, None] / float(max(TOKENS - 1, 1))
    rising = jnp.exp(math.log(3.0) * ramp)
    base = jnp.clip(jax.random.normal(first, (TOKENS, D), jnp.float32), -6.0, 6.0)
    return (0.3 * base * rising).astype(jnp.bfloat16)


def block_scale(own_key, dims, cuts, smallest, top_value):
    def one(dim, parts):
        steps = jax.random.uniform(jax.random.fold_in(jax.random.fold_in(own_key, 6), dim), (parts,), jnp.float32, smallest / len(cuts), top_value / len(cuts))
        return jnp.repeat(jnp.exp(steps), dims[dim] // parts).reshape((-1,) + (1,) * (len(dims) - dim - 1))

    gain = one(*cuts[0])
    for cut in cuts[1:]:
        gain = gain * one(*cut)
    return gain


def shared_out(own_key, own, number, rows, number_of, top, limit, lean):
    ranking = jax.random.permutation(own_key, number_of)
    heavy_load, usual = portions_of(number_of, rows * top, limit, lean, True), portions_of(number_of, rows * top, limit, lean, False)
    places = jnp.arange(number_of)

    def named(tallies, offset_by):
        used = int((tallies > 0).sum())
        fixed = max(1, used // 4)
        passed = fixed + (places - fixed + offset_by * (used - fixed)) % max(1, number_of - fixed)
        return jnp.zeros((number_of,), jnp.int32).at[ranking[jnp.where(places < fixed, places, passed)]].set(jnp.asarray(tallies, jnp.int32))

    tallies = jnp.where(number % 4 == 0, named(heavy_load, number // 4), named(usual, number - number // 4 - 1))
    mixed = jax.random.permutation(jax.random.fold_in(own, 3), number_of)
    source_of, receiver = mixed[0:number_of // 2 * 2:2], mixed[1:number_of // 2 * 2:2]
    slack = jnp.minimum(tallies[source_of] - 1, limit - tallies[receiver]) // 2
    slack = jnp.where((source_of == ranking[0]) | (receiver == ranking[0]) | (tallies[receiver] == 0), 0, jnp.maximum(slack, 0))
    passed = jax.random.randint(jax.random.fold_in(own, 4), (number_of // 2,), 0, 1 << 20) % (slack + 1)
    tallies = tallies.at[source_of].add(-passed).at[receiver].add(passed)
    labels = jnp.searchsorted(jnp.cumsum(tallies), jnp.arange(rows * top), side="right").astype(jnp.int32)
    listing = labels.reshape(top, rows).T
    listing = listing[jax.random.permutation(jax.random.fold_in(own, 1), rows)]
    offset_by = jax.random.randint(jax.random.fold_in(own, 2), (rows, 1), 0, top)
    return jnp.take_along_axis(listing, (jnp.arange(top)[None, :] + offset_by) % top, axis=1)


def portions_of(amount, total, reach, lean, full):
    portions = [(1 << 20) // math.isqrt(grade ** lean) + 1 for grade in range(1, amount + 1)]
    largest = reach if full else min(reach, max(-(-total // amount), total * portions[0] // sum(portions)))
    least = 1 if total - largest >= amount - 1 else 0
    counts, surplus = [largest] + [least] * (amount - 1), total - largest - least * (amount - 1)
    while surplus > 0:
        free = [i for i in range(1, amount) if counts[i] < largest] or [i for i in range(1, amount) if counts[i] < reach]
        whole, remaining = sum([portions[i] for i in free]), surplus
        for i in free:
            more = min(reach - counts[i], max(1, remaining * portions[i] // whole), surplus)
            counts[i] = counts[i] + more
            surplus = surplus - more
    return np.array(counts)


def scatter_about(key, extent, width, most, shards=(), kind=jnp.bfloat16):
    values = width * jax.random.normal(key, extent, jnp.float32)
    if shards:
        values = values * block_scale(key, extent, shards, -0.22, 0.18)
    return jnp.clip(values, -most, most).astype(kind)


def setup_inputs(seed: int = 0) -> dict:
    key_list = jax.random.split(jax.random.key(seed), 9)
    hidden = draw_hidden(jax.random.fold_in(key_list[8], 71), 0)
    norm_gain = jnp.clip(jnp.exp(jax.random.uniform(key_list[1], (D,), jnp.float32, math.log(0.5), math.log(2.0))), 0.5, 2.0)
    expert_ids_keys = jax.random.split(jax.random.fold_in(key_list[2], 1), TOKENS // ROWS_DEV)
    expert_ids_turns = jax.random.permutation(jax.random.fold_in(key_list[2], 3), TOKENS // ROWS_DEV)
    expert_ids = jax.vmap(lambda own, number: shared_out(jax.random.fold_in(key_list[2], 2), own, number, ROWS_DEV, EXPERTS, TOPK, CAP, 2))(expert_ids_keys, expert_ids_turns).reshape((TOKENS, TOPK))
    gate_probs = jnp.clip(jnp.exp(math.log(0.5) - 2.3025851 * jax.random.uniform(key_list[3], (TOKENS, TOPK), jnp.float32) ** block_scale(key_list[3], (TOKENS, TOPK), ((0, 32),), -0.2, 0.2)), 0.05, 0.5)
    out_grad = draw_out_grad(jax.random.fold_in(key_list[8], 71), 0)
    gate_weight = scatter_about(key_list[5], (EXPERTS, D, FF), D ** -0.5, 0.125, ((0, 32),))
    up_weight = scatter_about(key_list[6], (EXPERTS, D, FF), D ** -0.5, 0.125, ((0, 32),))
    down_weight = scatter_about(key_list[7], (EXPERTS, FF, D), FF ** -0.5, 0.21875, ((0, 32),))
    return {"hidden": hidden, "norm_gain": norm_gain, "expert_ids": expert_ids, "gate_probs": gate_probs, "out_grad": out_grad, "gate_weight": gate_weight, "up_weight": up_weight, "down_weight": down_weight}


epsilon = 1e-06

def reference(hidden, norm_gain, expert_ids, gate_probs, out_grad, gate_weight, up_weight, down_weight):
    values = hidden.astype(jnp.float32)
    inverse = lax.rsqrt(lax.optimization_barrier(jnp.mean(values * values, axis=-1, keepdims=True)) + epsilon)
    unit_rows = values * inverse
    normed = (unit_rows * norm_gain).astype(jnp.bfloat16)
    grad_rows = out_grad.astype(jnp.float32)
    scaled = (gate_probs[:, :, None] * grad_rows[:, None, :]).astype(jnp.bfloat16)
    total_pairs = TOKENS * TOPK
    flat_ids = expert_ids.reshape(-1).astype(jnp.int32)
    normed_pad = jnp.concatenate([normed, jnp.zeros((1, D), jnp.bfloat16)], axis=0)
    scaled_pad = jnp.concatenate([scaled.reshape(total_pairs, D), jnp.zeros((1, D), jnp.bfloat16)], axis=0)

    def single(operands):
        expert, w_gate, w_up, w_down = operands
        found = jnp.nonzero(flat_ids == expert, size=SLOTS, fill_value=total_pairs)[0].astype(jnp.int32)
        token = jnp.where(found < total_pairs, found // TOPK, TOKENS).astype(jnp.int32)
        inputs = normed_pad[token]
        cotan = scaled_pad[found]
        gate_pre = jnp.dot(inputs, w_gate, preferred_element_type=jnp.float32)
        up_pre = jnp.dot(inputs, w_up, preferred_element_type=jnp.float32)
        sigma = jax.nn.sigmoid(gate_pre)
        silu_vals = gate_pre * sigma
        act = (silu_vals * up_pre).astype(jnp.bfloat16)
        result = jnp.dot(act, w_down, preferred_element_type=jnp.float32).astype(jnp.bfloat16)
        act_grad = jnp.dot(cotan, w_down.T, preferred_element_type=jnp.float32)
        gate_pgrad = (act_grad * up_pre * sigma * (1.0 + gate_pre * (1.0 - sigma))).astype(jnp.bfloat16)
        up_pgrad = (act_grad * silu_vals).astype(jnp.bfloat16)
        down_g = jnp.dot(act.T, cotan, preferred_element_type=jnp.float32).astype(jnp.bfloat16)
        gate_g = jnp.dot(inputs.T, gate_pgrad, preferred_element_type=jnp.float32).astype(jnp.bfloat16)
        up_g = jnp.dot(inputs.T, up_pgrad, preferred_element_type=jnp.float32).astype(jnp.bfloat16)
        back = jnp.dot(gate_pgrad, w_gate.T, preferred_element_type=jnp.float32)
        back = back + jnp.dot(up_pgrad, w_up.T, preferred_element_type=jnp.float32)
        return (result, back.astype(jnp.bfloat16), found, gate_g, up_g, down_g)
    numbers = jnp.arange(EXPERTS, dtype=jnp.int32)
    results, backs, founds, gate_g, up_g, down_g = lax.map(single, (numbers, gate_weight, up_weight, down_weight))
    where_all = founds.reshape(-1).astype(jnp.int32)
    out_rows = jnp.zeros((total_pairs + 1, D), jnp.bfloat16).at[where_all].set(results.reshape(-1, D))
    out_rows = out_rows[:total_pairs].reshape(TOKENS, TOPK, D)
    back_rows = jnp.zeros((total_pairs + 1, D), jnp.bfloat16).at[where_all].set(backs.reshape(-1, D))
    back_rows = back_rows[:total_pairs].reshape(TOKENS, TOPK, D)
    out_f = out_rows.astype(jnp.float32)
    layer_out = (values + lax.optimization_barrier(jnp.sum(gate_probs[:, :, None] * out_f, axis=1))).astype(jnp.bfloat16)
    gate_grad = lax.optimization_barrier(jnp.sum(grad_rows[:, None, :] * out_f, axis=2))
    normed_total = lax.optimization_barrier(jnp.sum(back_rows.astype(jnp.float32), axis=1))
    gain_grad = lax.optimization_barrier(jnp.sum(normed_total * unit_rows, axis=0))
    upstream = normed_total * norm_gain
    input_grad = grad_rows + inverse * (upstream - unit_rows * lax.optimization_barrier(jnp.mean(upstream * unit_rows, axis=-1, keepdims=True)))
    return (layer_out, input_grad.astype(jnp.bfloat16), gate_grad, gain_grad, gate_g, up_g, down_g)
```

```python
import functools

import jax
import jax.numpy as jnp
from jax import lax
from jax.experimental import pallas as pl
from jax.experimental.pallas import tpu as pltpu
from jax.sharding import PartitionSpec as P

epsilon = 1e-06
AXES = ("dp", "tensor")
MESH = pl.DeviceIdType.MESH
f32, bf16 = jnp.float32, jnp.bfloat16


class Place:
    def __init__(self, line):
        self.line = line
        dp, tensor = lax.axis_index("dp"), lax.axis_index("tensor")
        self.z, self.x = dp // 2, dp % 2
        self.y, self.c = tensor // 2, tensor % 2

    def block(self, z, flip):
        x = 1 - self.x if flip in (1, 3) else self.x
        y = 1 - self.y if flip in (2, 3) else self.y
        return x, y

    def index(self, z, flip, c):
        x, y = self.block(z, flip)
        return (z * 2 + x) * 4 + y * 2 + c

    def device(self, z, flip, c):
        x, y = self.block(z, flip)
        return (z * 2 + x, y * 2 + c)

    def order(self, step, farthest_first):
        result = jnp.int32(0)
        for own in range(self.line):
            listed = sorted(range(self.line), key=lambda p: (abs(p - own), p))
            if farthest_first:
                listed = listed[::-1]
            result = jnp.where(self.z == own, jnp.int32(listed[step]), result)
        return result

    def greet(self):
        barrier = pltpu.get_barrier_semaphore()

        def tell(device):
            pl.semaphore_signal(barrier, inc=1, device_id=device, device_id_type=MESH)

        for flip, c in ((1, self.c), (2, self.c), (0, 1 - self.c)):
            tell(self.device(self.z, flip, c))
        below, above = self.z > 0, self.z < self.line - 1
        pl.when(below)(lambda: tell(self.device(self.z - 1, 0, self.c)))
        pl.when(above)(lambda: tell(self.device(self.z + 1, 0, self.c)))
        pl.semaphore_wait(barrier, 3 + below.astype(jnp.int32) + above.astype(jnp.int32))


UP, DOWN, SIDE, FACE, HALF0, HALF1, CORE = 0, 1, 2, 3, 4, 5, 6


class Gather:
    def __init__(self, place, own, held, send, recv, keep):
        self.p, self.own, self.held = place, own, held
        self.send, self.recv, self.keep = send, recv, keep
        self.half = own.shape[0] // 2

    def copy(self, kind, zz, flip, part, device, own=False):
        where = self.p.index(zz, flip, self.p.c)
        dst = self.held.at[where]
        src = self.own if own else dst
        if part is not None:
            rows = pl.ds(part * self.half, self.half)
            src, dst = src.at[rows], dst.at[rows]
        return pltpu.make_async_remote_copy(
            src_ref=src, dst_ref=dst, send_sem=self.send.at[kind, zz],
            recv_sem=self.recv.at[kind, zz], device_id=device, device_id_type=MESH,
        )

    def up(self, zz, own=False):
        return self.copy(UP, zz, 0, None, self.p.device(self.p.z + 1, 0, self.p.c), own)

    def down(self, zz, own=False):
        return self.copy(DOWN, zz, 0, None, self.p.device(self.p.z - 1, 0, self.p.c), own)

    def side(self, zz, own=False):
        return self.copy(SIDE, zz, 0, None, self.p.device(self.p.z, 1, self.p.c), own)

    def face(self, zz, own=False):
        return self.copy(FACE, zz, 0, None, self.p.device(self.p.z, 2, self.p.c), own)

    def half0(self, zz):
        return self.copy(HALF0, zz, 1, 0, self.p.device(self.p.z, 2, self.p.c))

    def half1(self, zz):
        return self.copy(HALF1, zz, 2, 1, self.p.device(self.p.z, 1, self.p.c))

    def core(self, zz, flip, own=False):
        return self.copy(CORE + flip, zz, flip, None, self.p.device(self.p.z, 0, 1 - self.p.c), own)

    def arrived(self, kind, zz, flip, part, c=None):
        where = self.p.index(zz, flip, self.p.c if c is None else c)
        dst = self.held.at[where]
        if part is not None:
            dst = dst.at[pl.ds(part * self.half, self.half)]
        pltpu.make_async_remote_copy(
            src_ref=dst, dst_ref=dst, send_sem=self.send.at[kind, zz],
            recv_sem=self.recv.at[kind, zz],
            device_id=self.p.device(self.p.z, 0, 1 - self.p.c), device_id_type=MESH,
        ).wait_recv()

    def first(self):
        p = self.p
        pltpu.make_async_copy(self.own, self.held.at[p.index(p.z, 0, p.c)], self.keep).start()
        pl.when(p.z < p.line - 1)(lambda: self.up(p.z, True).start())
        pl.when(p.z > 0)(lambda: self.down(p.z, True).start())
        self.side(p.z, True).start()
        self.face(p.z, True).start()
        self.core(p.z, 0, True).start()

    def column(self, step):
        p, zz = self.p, self.p.order(step, False)

        @pl.when(zz < p.z)
        def _():
            self.arrived(UP, zz, 0, None)
            pl.when(p.z < p.line - 1)(lambda: self.up(zz).start())

        @pl.when(zz > p.z)
        def _():
            self.arrived(DOWN, zz, 0, None)
            pl.when(p.z > 0)(lambda: self.down(zz).start())

        self.side(zz).start()
        self.face(zz).start()
        self.core(zz, 0).start()

    def plane(self, step):
        zz = self.p.order(step, False)
        self.arrived(SIDE, zz, 1, None)
        self.half0(zz).start()
        self.core(zz, 1).start()
        self.arrived(FACE, zz, 2, None)
        self.half1(zz).start()
        self.core(zz, 2).start()

    def corner(self, step):
        zz = self.p.order(step, False)
        self.arrived(HALF0, zz, 3, 0)
        self.arrived(HALF1, zz, 3, 1)
        self.core(zz, 3).start()

    def slot(self, step):
        line = self.p.line
        if step == 0:
            self.first()
        elif 0 < step < line:
            self.column(step)
        if 0 <= step - 1 < line:
            self.plane(step - 1)
        if 0 <= step - 2 < line:
            self.corner(step - 2)

    def finish(self):
        p = self.p
        for zz in range(p.line):
            for flip in range(4):
                self.arrived(CORE + flip, zz, flip, None, 1 - p.c)
        for zz in range(p.line):
            pl.when((zz <= p.z) & (p.z < p.line - 1))(lambda zz=zz: self.up(zz).wait_send())
            pl.when((zz >= p.z) & (p.z > 0))(lambda zz=zz: self.down(zz).wait_send())
            for one in (self.side(zz), self.face(zz), self.half0(zz), self.half1(zz)):
                one.wait_send()
            for flip in range(4):
                self.core(zz, flip).wait_send()
        pltpu.make_async_copy(self.own, self.held.at[p.index(p.z, 0, p.c)], self.keep).wait()


def gather_kernel(line, offsets, *refs):
    count = len(offsets)
    owns, helds = refs[:count], refs[count:2 * count]
    send, recv, keep = refs[2 * count:]
    place = Place(line)
    place.greet()
    arrays = [
        Gather(place, owns[i], helds[i], send.at[i], recv.at[i], keep.at[i]) for i in range(count)
    ]
    for step in range(max(offsets) + line + 2):
        for one, offset in zip(arrays, offsets):
            one.slot(step - offset)
    for one in arrays:
        one.finish()


def gather_all(arrays, offsets, number):
    line = lax.axis_size("dp") // 2
    devices = lax.axis_size(AXES)
    count = len(arrays)
    return pl.pallas_call(
        functools.partial(gather_kernel, line, offsets),
        out_shape=[jax.ShapeDtypeStruct((devices,) + a.shape, a.dtype) for a in arrays],
        in_specs=[pl.BlockSpec(memory_space=pltpu.VMEM)] * count,
        out_specs=[pl.BlockSpec(memory_space=pl.ANY)] * count,
        scratch_shapes=[
            pltpu.SemaphoreType.DMA((count, 10, line)),
            pltpu.SemaphoreType.DMA((count, 10, line)),
            pltpu.SemaphoreType.DMA((count,)),
        ],
        compiler_params=pltpu.CompilerParams(collective_id=number, has_side_effects=True),
        name=f"gather{number}",
    )(*arrays)


def add_rows(start, count, store, *loads):
    chunk = 16

    @pl.loop(0, count // chunk)
    def _(i):
        rows = pl.ds(pl.multiple_of(start + i * chunk, chunk), chunk)
        total = loads[0](rows).astype(f32)
        for load in loads[1:]:
            total = total + load(rows).astype(f32)
        store(rows, total)


def scatter_kernel(
    line, part, out, mine, theirs, half_in, side_in, face_in, up_in, down_in,
    send, recv, keep,
):
    p = Place(line)
    p.greet()
    count = out.shape[0]
    half = count // 2
    z = p.z

    def put(ref, index):
        def store(rows, value):
            ref[index + (rows,)] = value.astype(ref.dtype)
        return store

    def get(ref, index):
        return lambda rows: ref[index + (rows,)]

    def remote(src, dst, kind, zz, device):
        return pltpu.make_async_remote_copy(
            src_ref=src, dst_ref=dst, send_sem=send.at[kind, zz], recv_sem=recv.at[kind, zz],
            device_id=device, device_id_type=MESH,
        )

    def core(zz, flip):
        return remote(
            part.at[p.index(zz, flip, 1 - p.c)], theirs.at[zz, flip], CORE + flip, zz,
            p.device(z, 0, 1 - p.c),
        )

    def load(zz, flip):
        return pltpu.make_async_copy(
            part.at[p.index(zz, flip, p.c)], mine.at[zz, flip], keep.at[flip, zz]
        )

    def half0(zz):
        return remote(
            theirs.at[zz, 3, pl.ds(0, half)], half_in.at[zz, 0], HALF0, zz, p.device(z, 2, p.c)
        )

    def half1(zz):
        return remote(
            theirs.at[zz, 3, pl.ds(half, half)], half_in.at[zz, 1], HALF1, zz, p.device(z, 1, p.c)
        )

    def side(zz):
        return remote(theirs.at[zz, 1], side_in.at[zz], SIDE, zz, p.device(z, 1, p.c))

    def face(zz):
        return remote(theirs.at[zz, 2], face_in.at[zz], FACE, zz, p.device(z, 2, p.c))

    def up(zz):
        return remote(theirs.at[zz, 0], up_in.at[zz], UP, zz, p.device(z + 1, 0, p.c))

    def down(zz):
        return remote(theirs.at[zz, 0], down_in.at[zz], DOWN, zz, p.device(z - 1, 0, p.c))

    def joined(zz, flip):
        core(zz, flip).wait_recv()
        load(zz, flip).wait()
        add_rows(
            0, count, put(theirs, (zz, flip)), get(theirs, (zz, flip)), get(mine, (zz, flip))
        )

    for step in range(line):
        zz = p.order(step, True)
        for flip in (3, 1, 2, 0):
            core(zz, flip).start()
            load(zz, flip).start()

    def corner(step):
        zz = p.order(step, True)
        joined(zz, 3)
        half0(zz).start()
        half1(zz).start()
        for flip in (1, 2, 0):
            joined(zz, flip)

    def plane(step):
        zz = p.order(step, True)
        half0(zz).wait_recv()
        here = (zz, 1)
        add_rows(
            0, half, put(theirs, here), get(theirs, here), get(half_in, (zz, 0))
        )
        side(zz).start()
        half1(zz).wait_recv()

        @pl.loop(0, half // 16)
        def _(i):
            low = pl.ds(pl.multiple_of(i * 16, 16), 16)
            high = pl.ds(pl.multiple_of(half + i * 16, 16), 16)
            total = theirs[zz, 2, high].astype(f32) + half_in[zz, 1, low].astype(f32)
            theirs[zz, 2, high] = total.astype(bf16)

        face(zz).start()

    def column(step):
        zz = p.order(step, True)
        side(zz).wait_recv()
        face(zz).wait_recv()
        base = (get(theirs, (zz, 0)), get(side_in, (zz,)), get(face_in, (zz,)))
        if step == line - 1:
            add_rows(0, count, put(out, ()), *base)

            @pl.when(z > 0)
            def _():
                up(zz).wait_recv()
                add_rows(0, count, put(out, ()), get(out, ()), get(up_in, (zz,)))

            @pl.when(z < line - 1)
            def _():
                down(zz).wait_recv()
                add_rows(0, count, put(out, ()), get(out, ()), get(down_in, (zz,)))

            return

        def onward(copy, source, more):
            @pl.when(more)
            def _():
                copy(zz).wait_recv()
                add_rows(0, count, put(theirs, (zz, 0)), *base, get(source, (zz,)))

            @pl.when(jnp.logical_not(more))
            def _():
                add_rows(0, count, put(theirs, (zz, 0)), *base)

            copy(zz).start()

        pl.when(zz > z)(lambda: onward(up, up_in, z > 0))
        pl.when(zz < z)(lambda: onward(down, down_in, z < line - 1))

    for step in range(line + 2):
        if step < line:
            corner(step)
        if 0 <= step - 1 < line:
            plane(step - 1)
        if 0 <= step - 2 < line:
            column(step - 2)

    for zz in range(line):
        for flip in range(4):
            core(zz, flip).wait_send()
        for one in (half0, half1, side, face):
            one(zz).wait_send()
        pl.when(zz > z)(lambda zz=zz: up(zz).wait_send())
        pl.when(zz < z)(lambda zz=zz: down(zz).wait_send())


def scatter_sum(part, number):
    line = lax.axis_size("dp") // 2
    _, rows, width = part.shape
    return pl.pallas_call(
        functools.partial(scatter_kernel, line),
        out_shape=jax.ShapeDtypeStruct((rows, width), f32),
        in_specs=[pl.BlockSpec(memory_space=pl.ANY)],
        out_specs=pl.BlockSpec(memory_space=pltpu.VMEM),
        scratch_shapes=[
            pltpu.VMEM((line, 4, rows, width), bf16),
            pltpu.VMEM((line, 4, rows, width), bf16),
            pltpu.VMEM((line, 2, rows // 2, width), bf16),
            pltpu.VMEM((line, rows, width), bf16),
            pltpu.VMEM((line, rows, width), bf16),
            pltpu.VMEM((line, rows, width), bf16),
            pltpu.VMEM((line, rows, width), bf16),
            pltpu.SemaphoreType.DMA((10, line)),
            pltpu.SemaphoreType.DMA((10, line)),
            pltpu.SemaphoreType.DMA((4, line)),
        ],
        compiler_params=pltpu.CompilerParams(
            collective_id=number, has_side_effects=True, vmem_limit_bytes=60 * 2**20
        ),
        name=f"scatter{number}",
    )(part)


def last_kernel(line, small, grad, held, rows_out, send, recv, keep, tsend, trecv, tkeep):
    p = Place(line)
    p.greet()
    here = p.y * 2 + p.c
    other = (1 - p.y) * 2 + p.c

    def tremote(src, where, i, device):
        return pltpu.make_async_remote_copy(
            src_ref=src, dst_ref=rows_out.at[where], send_sem=tsend.at[i], recv_sem=trecv.at[i],
            device_id=device, device_id_type=MESH,
        )

    partner = p.device(p.z, 0, 1 - p.c)
    keeping = pltpu.make_async_copy(grad, rows_out.at[here], tkeep)
    keeping.start()
    across = tremote(grad, here, 0, p.device(p.z, 2, p.c))
    beside = tremote(grad, here, 1, partner)
    relay = tremote(rows_out.at[other], other, 2, partner)
    across.start()
    beside.start()
    one = Gather(p, small, held, send, recv, keep)
    for step in range(line + 2):
        one.slot(step)
        if step == 1:
            across.wait_recv()
            relay.start()
    one.finish()
    beside.wait_recv()
    relay.wait_recv()
    for copy in (across, beside, relay):
        copy.wait_send()
    keeping.wait()


def gather_last(small, grad, number):
    line = lax.axis_size("dp") // 2
    devices, quarters = lax.axis_size(AXES), lax.axis_size("tensor")
    anywhere = pl.BlockSpec(memory_space=pl.ANY)
    return pl.pallas_call(
        functools.partial(last_kernel, line),
        out_shape=[
            jax.ShapeDtypeStruct((devices,) + small.shape, small.dtype),
            jax.ShapeDtypeStruct((quarters,) + grad.shape, grad.dtype),
        ],
        in_specs=[pl.BlockSpec(memory_space=pltpu.VMEM)] * 2,
        out_specs=[anywhere, anywhere],
        scratch_shapes=[
            pltpu.SemaphoreType.DMA((10, line)),
            pltpu.SemaphoreType.DMA((10, line)),
            pltpu.SemaphoreType.DMA,
            pltpu.SemaphoreType.DMA((3,)),
            pltpu.SemaphoreType.DMA((3,)),
            pltpu.SemaphoreType.DMA,
        ],
        compiler_params=pltpu.CompilerParams(collective_id=number, has_side_effects=True),
        name=f"last{number}",
    )(small, grad)


def per_device(
    hidden, norm_gain, expert_ids, gate_probs, out_grad, gate_weight, up_weight, down_weight
):
    quarters = lax.axis_size("tensor")
    quarter = lax.axis_index("tensor")
    own_count = hidden.shape[0] // quarters
    width = hidden.shape[1]
    top_count = expert_ids.shape[1]
    devices = lax.axis_size(AXES)
    experts = gate_weight.shape[0] * devices
    capacity = 2 * own_count * top_count // experts
    tokens = own_count * devices
    blocks_in = min(4, devices)
    groups = devices // blocks_in
    gtok = own_count * blocks_in
    gslots = capacity * blocks_in
    slots = groups * gslots
    me = lax.axis_index(AXES)

    own_rows = lax.dynamic_slice_in_dim(hidden, quarter * own_count, own_count, 0)
    values = own_rows.astype(f32)
    inverse = lax.rsqrt(jnp.mean(values * values, axis=-1, keepdims=True) + epsilon)
    unit_rows = values * inverse
    normed = (unit_rows * norm_gain).astype(bf16)
    grad_rows = out_grad.astype(f32)

    meta = jnp.concatenate(
        [
            expert_ids.astype(f32),
            gate_probs,
            jnp.zeros((own_count, 128 - 2 * top_count), f32),
        ],
        axis=1,
    )
    meta_all, normed_all, grads_all = gather_all(
        [meta, normed, out_grad], (0, 0, lax.axis_size("dp") // 2 - 1), 0
    )
    meta_all = meta_all.reshape(tokens, 128)
    ids_all = meta_all[:, :top_count].astype(jnp.int32)
    probs_all = meta_all[:, top_count:2 * top_count]

    hits = ids_all == me
    member = jnp.any(hits, axis=1).reshape(devices, own_count)
    prob = jnp.sum(jnp.where(hits, probs_all, 0.0), axis=1)
    place = jnp.cumsum(member.astype(jnp.int32), axis=1) - 1
    block = jnp.arange(devices, dtype=jnp.int32)[:, None] % blocks_in
    slot = jnp.where(member, block * capacity + place, -1).reshape(groups, gtok)
    picks = slot[:, None, :] == jnp.arange(gslots, dtype=jnp.int32)[None, :, None]
    choose = picks.astype(bf16)
    slot_prob = jnp.sum(
        jnp.where(picks, prob.reshape(groups, 1, gtok), 0.0), axis=2
    ).reshape(slots, 1)

    def pack(rows):
        return jnp.einsum(
            "gst,gtd->gsd", choose, rows.reshape(groups, gtok, width), preferred_element_type=f32
        ).astype(bf16).reshape(slots, width)

    def spread(rows):
        return jnp.einsum(
            "gst,gsd->gtd", choose, rows.reshape(groups, gslots, width), preferred_element_type=f32
        ).astype(bf16).reshape(devices, own_count, width)

    def dot(a, b, ca, cb):
        return lax.dot_general(a, b, (((ca,), (cb,)), ((), ())), preferred_element_type=f32)

    w_gate, w_up, w_down = gate_weight[0], up_weight[0], down_weight[0]
    inputs = pack(normed_all)
    gate_pre = dot(inputs, w_gate, 1, 0)
    up_pre = dot(inputs, w_up, 1, 0)
    sigma = jax.nn.sigmoid(gate_pre)
    silu_vals = gate_pre * sigma
    act = (silu_vals * up_pre).astype(bf16)
    results = dot(act, w_down, 1, 0).astype(bf16)
    results_f = results.astype(f32)
    layer_part = scatter_sum(spread((slot_prob * results_f).astype(bf16)), 1)

    grads = pack(grads_all).astype(f32)
    cotan = (slot_prob * grads).astype(bf16)
    slot_gg = jnp.sum(grads * results_f, axis=1)
    act_grad = dot(cotan, w_down, 1, 1)
    gate_pgrad = (act_grad * up_pre * sigma * (1.0 + gate_pre * (1.0 - sigma))).astype(bf16)
    up_pgrad = (act_grad * silu_vals).astype(bf16)
    back = dot(gate_pgrad, w_gate, 1, 1) + dot(up_pgrad, w_up, 1, 1)
    normed_total = scatter_sum(spread(back.astype(bf16)), 2)
    token_gg = jnp.sum(jnp.where(picks, slot_gg.reshape(groups, gslots, 1), 0.0), axis=1)

    down_grad = dot(act, cotan, 0, 0).astype(bf16)[None]
    gate_wgrad = dot(inputs, gate_pgrad, 0, 0).astype(bf16)[None]
    up_wgrad = dot(inputs, up_pgrad, 0, 0).astype(bf16)[None]

    layer_out = (values + layer_part).astype(bf16)
    gain_part = jnp.sum(normed_total * unit_rows, axis=0)
    upstream = normed_total * norm_gain
    own_grad = grad_rows + inverse * (
        upstream - unit_rows * jnp.mean(upstream * unit_rows, axis=-1, keepdims=True)
    )
    small = jnp.concatenate([token_gg.reshape(-1, 128), gain_part.reshape(-1, 128)], axis=0)
    small_all, input_grad = gather_last(small, own_grad.astype(bf16), 3)
    input_grad = input_grad.reshape(hidden.shape)
    tiles = tokens // 128
    gain_grad = jnp.sum(small_all[:, tiles:, :], axis=0).reshape(width)
    mine = lax.dynamic_slice_in_dim(
        small_all[:, :tiles, :].reshape(devices, tokens), me * own_count, own_count, 1
    )
    named = expert_ids[:, :, None] == jnp.arange(devices, dtype=jnp.int32)[None, None, :]
    gate_grad = jnp.sum(jnp.where(named, mine.T[:, None, :], 0.0), axis=2)
    return (layer_out, input_grad, gate_grad, gain_grad, gate_wgrad, up_wgrad, down_grad)


def solution(mesh):
    rows, wide = P(AXES, None), P(AXES, None, None)
    in_specs = (P("dp", None), P(), rows, rows, rows, wide, wide, wide)
    out_specs = (rows, P("dp", None), rows, P(), wide, wide, wide)
    return jax.shard_map(
        per_device, mesh=mesh, in_specs=in_specs, out_specs=out_specs, check_vma=False
    )
```

```python
import functools

import jax
import jax.numpy as jnp
from jax import lax
from jax.experimental import pallas as pl
from jax.experimental.pallas import tpu as pltpu
from jax.sharding import PartitionSpec as P

epsilon = 1e-06
AXES = ("dp", "tensor")
MESH = pl.DeviceIdType.MESH
f32, bf16 = jnp.float32, jnp.bfloat16


class Place:
    def __init__(self, line):
        self.line = line
        dp, tensor = lax.axis_index("dp"), lax.axis_index("tensor")
        self.z, self.x = dp // 2, dp % 2
        self.y, self.c = tensor // 2, tensor % 2

    def block(self, z, flip):
        x = 1 - self.x if flip in (1, 3) else self.x
        y = 1 - self.y if flip in (2, 3) else self.y
        return x, y

    def index(self, z, flip, c):
        x, y = self.block(z, flip)
        return (z * 2 + x) * 4 + y * 2 + c

    def device(self, z, flip, c):
        x, y = self.block(z, flip)
        return (z * 2 + x, y * 2 + c)

    def order(self, step, farthest_first):
        result = jnp.int32(0)
        for own in range(self.line):
            listed = sorted(range(self.line), key=lambda p: (abs(p - own), p))
            if farthest_first:
                listed = listed[::-1]
            result = jnp.where(self.z == own, jnp.int32(listed[step]), result)
        return result

    def greet(self):
        barrier = pltpu.get_barrier_semaphore()

        def tell(device):
            pl.semaphore_signal(barrier, inc=1, device_id=device, device_id_type=MESH)

        for flip, c in ((1, self.c), (2, self.c), (0, 1 - self.c)):
            tell(self.device(self.z, flip, c))
        below, above = self.z > 0, self.z < self.line - 1
        pl.when(below)(lambda: tell(self.device(self.z - 1, 0, self.c)))
        pl.when(above)(lambda: tell(self.device(self.z + 1, 0, self.c)))
        pl.semaphore_wait(barrier, 3 + below.astype(jnp.int32) + above.astype(jnp.int32))


UP, DOWN, SIDE, FACE, HALF0, HALF1, CORE = 0, 1, 2, 3, 4, 5, 6


class Gather:
    def __init__(self, place, own, held, send, recv, keep):
        self.p, self.own, self.held = place, own, held
        self.send, self.recv, self.keep = send, recv, keep
        self.half = own.shape[0] // 2

    def copy(self, kind, zz, flip, part, device, own=False):
        where = self.p.index(zz, flip, self.p.c)
        dst = self.held.at[where]
        src = self.own if own else dst
        if part is not None:
            rows = pl.ds(part * self.half, self.half)
            src, dst = src.at[rows], dst.at[rows]
        return pltpu.make_async_remote_copy(
            src_ref=src, dst_ref=dst, send_sem=self.send.at[kind, zz],
            recv_sem=self.recv.at[kind, zz], device_id=device, device_id_type=MESH,
        )

    def up(self, zz, own=False):
        return self.copy(UP, zz, 0, None, self.p.device(self.p.z + 1, 0, self.p.c), own)

    def down(self, zz, own=False):
        return self.copy(DOWN, zz, 0, None, self.p.device(self.p.z - 1, 0, self.p.c), own)

    def side(self, zz, own=False):
        return self.copy(SIDE, zz, 0, None, self.p.device(self.p.z, 1, self.p.c), own)

    def face(self, zz, own=False):
        return self.copy(FACE, zz, 0, None, self.p.device(self.p.z, 2, self.p.c), own)

    def half0(self, zz):
        return self.copy(HALF0, zz, 1, 0, self.p.device(self.p.z, 2, self.p.c))

    def half1(self, zz):
        return self.copy(HALF1, zz, 2, 1, self.p.device(self.p.z, 1, self.p.c))

    def core(self, zz, flip, own=False):
        return self.copy(CORE + flip, zz, flip, None, self.p.device(self.p.z, 0, 1 - self.p.c), own)

    def arrived(self, kind, zz, flip, part, c=None):
        where = self.p.index(zz, flip, self.p.c if c is None else c)
        dst = self.held.at[where]
        if part is not None:
            dst = dst.at[pl.ds(part * self.half, self.half)]
        pltpu.make_async_remote_copy(
            src_ref=dst, dst_ref=dst, send_sem=self.send.at[kind, zz],
            recv_sem=self.recv.at[kind, zz],
            device_id=self.p.device(self.p.z, 0, 1 - self.p.c), device_id_type=MESH,
        ).wait_recv()

    def first(self):
        p = self.p
        pltpu.make_async_copy(self.own, self.held.at[p.index(p.z, 0, p.c)], self.keep).start()
        pl.when(p.z < p.line - 1)(lambda: self.up(p.z, True).start())
        pl.when(p.z > 0)(lambda: self.down(p.z, True).start())
        self.side(p.z, True).start()
        self.face(p.z, True).start()
        self.core(p.z, 0, True).start()

    def column(self, step):
        p, zz = self.p, self.p.order(step, False)

        @pl.when(zz < p.z)
        def _():
            self.arrived(UP, zz, 0, None)
            pl.when(p.z < p.line - 1)(lambda: self.up(zz).start())

        @pl.when(zz > p.z)
        def _():
            self.arrived(DOWN, zz, 0, None)
            pl.when(p.z > 0)(lambda: self.down(zz).start())

        self.side(zz).start()
        self.face(zz).start()
        self.core(zz, 0).start()

    def plane(self, step):
        zz = self.p.order(step, False)
        self.arrived(SIDE, zz, 1, None)
        self.half0(zz).start()
        self.core(zz, 1).start()
        self.arrived(FACE, zz, 2, None)
        self.half1(zz).start()
        self.core(zz, 2).start()

    def corner(self, step):
        zz = self.p.order(step, False)
        self.arrived(HALF0, zz, 3, 0)
        self.arrived(HALF1, zz, 3, 1)
        self.core(zz, 3).start()

    def slot(self, step):
        line = self.p.line
        if step == 0:
            self.first()
        elif 0 < step < line:
            self.column(step)
        if 0 <= step - 1 < line:
            self.plane(step - 1)
        if 0 <= step - 2 < line:
            self.corner(step - 2)

    def finish(self):
        p = self.p
        for zz in range(p.line):
            for flip in range(4):
                self.arrived(CORE + flip, zz, flip, None, 1 - p.c)
        for zz in range(p.line):
            pl.when((zz <= p.z) & (p.z < p.line - 1))(lambda zz=zz: self.up(zz).wait_send())
            pl.when((zz >= p.z) & (p.z > 0))(lambda zz=zz: self.down(zz).wait_send())
            for one in (self.side(zz), self.face(zz), self.half0(zz), self.half1(zz)):
                one.wait_send()
            for flip in range(4):
                self.core(zz, flip).wait_send()
        pltpu.make_async_copy(self.own, self.held.at[p.index(p.z, 0, p.c)], self.keep).wait()


def gather_kernel(line, offsets, *refs):
    count = len(offsets)
    owns, helds = refs[:count], refs[count:2 * count]
    send, recv, keep = refs[2 * count:]
    place = Place(line)
    place.greet()
    arrays = [
        Gather(place, owns[i], helds[i], send.at[i], recv.at[i], keep.at[i]) for i in range(count)
    ]
    for step in range(max(offsets) + line + 2):
        for one, offset in zip(arrays, offsets):
            one.slot(step - offset)
    for one in arrays:
        one.finish()


def gather_all(arrays, offsets, number):
    line = lax.axis_size("dp") // 2
    devices = lax.axis_size(AXES)
    count = len(arrays)
    return pl.pallas_call(
        functools.partial(gather_kernel, line, offsets),
        out_shape=[jax.ShapeDtypeStruct((devices,) + a.shape, a.dtype) for a in arrays],
        in_specs=[pl.BlockSpec(memory_space=pltpu.VMEM)] * count,
        out_specs=[pl.BlockSpec(memory_space=pl.ANY)] * count,
        scratch_shapes=[
            pltpu.SemaphoreType.DMA((count, 10, line)),
            pltpu.SemaphoreType.DMA((count, 10, line)),
            pltpu.SemaphoreType.DMA((count,)),
        ],
        compiler_params=pltpu.CompilerParams(collective_id=number, has_side_effects=True),
        name=f"gather{number}",
    )(*arrays)


def add_rows(start, count, store, *loads):
    chunk = 16

    @pl.loop(0, count // chunk)
    def _(i):
        rows = pl.ds(pl.multiple_of(start + i * chunk, chunk), chunk)
        total = loads[0](rows).astype(f32)
        for load in loads[1:]:
            total = total + load(rows).astype(f32)
        store(rows, total)


def dot(a, b, ca, cb):
    return lax.dot_general(a, b, (((ca,), (cb,)), ((), ())), preferred_element_type=f32)


def row_grads(act_grad, gate_pre, up_pre):
    sigma = jax.nn.sigmoid(gate_pre)
    gate_pgrad = act_grad * up_pre * sigma * (1.0 + gate_pre * (1.0 - sigma))
    return gate_pgrad.astype(bf16), (act_grad * (gate_pre * sigma)).astype(bf16)


def backward_plain(cotan, gate_pre, up_pre, w_down, w_gate, w_up):
    gate_pgrad, up_pgrad = row_grads(dot(cotan, w_down, 1, 1), gate_pre, up_pre)
    back = dot(gate_pgrad, w_gate, 1, 1) + dot(up_pgrad, w_up, 1, 1)
    return gate_pgrad, up_pgrad, back.astype(bf16)


def backward_tile(step, ready, ins, outs):
    cotan, gate_pre, up_pre, w_down, w_gate, w_up = ins
    gate_pgrad, up_pgrad, back = outs
    if step == 0:
        ready(0, 1, 2, 3)
    count = cotan.shape[0] // 4
    rows = pl.ds(step * count, count)
    one, two = row_grads(dot(cotan[rows], w_down[...], 1, 1), gate_pre[rows], up_pre[rows])
    gate_pgrad[rows] = one
    up_pgrad[rows] = two
    if step == 0:
        ready(4, 5)
    wide = 512

    @pl.loop(0, back.shape[1] // wide)
    def _(i):
        cols = pl.ds(pl.multiple_of(i * wide, wide), wide)
        total = dot(gate_pgrad[rows], w_gate[cols], 1, 1) + dot(up_pgrad[rows], w_up[cols], 1, 1)
        back[rows, cols] = total.astype(bf16)


def weights_plain(inputs, gate_pgrad, up_pgrad, act, cotan):
    return tuple(
        dot(a, b, 0, 0).astype(bf16)
        for a, b in ((inputs, gate_pgrad), (inputs, up_pgrad), (act, cotan))
    )


def weights_tile(step, ready, ins, outs):
    inputs, gate_pgrad, up_pgrad, act, cotan = ins
    gate_wgrad, up_wgrad, down_grad = outs
    if step == 0:
        ready(0, 1, 2)
    deep, wide = 256, 512
    share = inputs.shape[1] // deep // 4

    @pl.loop(step * share, (step + 1) * share)
    def _(i):
        cols = pl.ds(pl.multiple_of(i * deep, deep), deep)
        block = inputs[:, cols]
        gate_wgrad[cols] = dot(block, gate_pgrad[...], 0, 0).astype(bf16)
        up_wgrad[cols] = dot(block, up_pgrad[...], 0, 0).astype(bf16)

    if step == 0:
        ready(3, 4)
    if step * deep < act.shape[1]:
        rows = pl.ds(step * deep, deep)

        @pl.loop(0, cotan.shape[1] // wide)
        def _(i):
            cols = pl.ds(pl.multiple_of(i * wide, wide), wide)
            down_grad[rows, cols] = dot(act[:, rows], cotan[:, cols], 0, 0).astype(bf16)


def scatter_kernel(line, job, n_in, n_out, *refs):
    part, refs = refs[0], refs[1:]
    job_in, refs = refs[:n_in], refs[n_in:]
    out, refs = refs[0], refs[1:]
    job_out, refs = refs[:n_out], refs[n_out:]
    mine, theirs, half_in, side_in, face_in, up_in, down_in, send, recv, keep = refs[:10]
    held_in, held_out = refs[10:10 + n_in], refs[10 + n_in:10 + n_in + n_out]
    if job is not None:
        in_sem, out_sem = refs[10 + n_in + n_out:]
        arriving = [
            pltpu.make_async_copy(job_in[i], held_in[i], in_sem.at[i]) for i in range(n_in)
        ]
        leaving = [
            pltpu.make_async_copy(held_out[i], job_out[i], out_sem.at[i]) for i in range(n_out)
        ]

    def ready(*which):
        for i in which:
            arriving[i].wait()

    p = Place(line)
    p.greet()
    count = out.shape[0]
    half = count // 2
    z = p.z

    def put(ref, index):
        def store(rows, value):
            ref[index + (rows,)] = value.astype(ref.dtype)
        return store

    def get(ref, index):
        return lambda rows: ref[index + (rows,)]

    def remote(src, dst, kind, zz, device):
        return pltpu.make_async_remote_copy(
            src_ref=src, dst_ref=dst, send_sem=send.at[kind, zz], recv_sem=recv.at[kind, zz],
            device_id=device, device_id_type=MESH,
        )

    def core(zz, flip):
        return remote(
            part.at[p.index(zz, flip, 1 - p.c)], theirs.at[zz, flip], CORE + flip, zz,
            p.device(z, 0, 1 - p.c),
        )

    def load(zz, flip):
        return pltpu.make_async_copy(
            part.at[p.index(zz, flip, p.c)], mine.at[zz, flip], keep.at[flip, zz]
        )

    def half0(zz):
        return remote(
            theirs.at[zz, 3, pl.ds(0, half)], half_in.at[zz, 0], HALF0, zz, p.device(z, 2, p.c)
        )

    def half1(zz):
        return remote(
            theirs.at[zz, 3, pl.ds(half, half)], half_in.at[zz, 1], HALF1, zz, p.device(z, 1, p.c)
        )

    def side(zz):
        return remote(theirs.at[zz, 1], side_in.at[zz], SIDE, zz, p.device(z, 1, p.c))

    def face(zz):
        return remote(theirs.at[zz, 2], face_in.at[zz], FACE, zz, p.device(z, 2, p.c))

    def up(zz):
        return remote(theirs.at[zz, 0], up_in.at[zz], UP, zz, p.device(z + 1, 0, p.c))

    def down(zz):
        return remote(theirs.at[zz, 0], down_in.at[zz], DOWN, zz, p.device(z - 1, 0, p.c))

    def joined(zz, flip):
        core(zz, flip).wait_recv()
        load(zz, flip).wait()
        add_rows(
            0, count, put(theirs, (zz, flip)), get(theirs, (zz, flip)), get(mine, (zz, flip))
        )

    for step in range(line):
        zz = p.order(step, True)
        for flip in (3, 1, 2, 0):
            core(zz, flip).start()
            load(zz, flip).start()

    if job is not None:
        for copy in arriving:
            copy.start()

    def corner(step):
        zz = p.order(step, True)
        joined(zz, 3)
        half0(zz).start()
        half1(zz).start()
        for flip in (1, 2, 0):
            joined(zz, flip)

    def plane(step):
        zz = p.order(step, True)
        half0(zz).wait_recv()
        here = (zz, 1)
        add_rows(
            0, half, put(theirs, here), get(theirs, here), get(half_in, (zz, 0))
        )
        side(zz).start()
        half1(zz).wait_recv()

        @pl.loop(0, half // 16)
        def _(i):
            low = pl.ds(pl.multiple_of(i * 16, 16), 16)
            high = pl.ds(pl.multiple_of(half + i * 16, 16), 16)
            total = theirs[zz, 2, high].astype(f32) + half_in[zz, 1, low].astype(f32)
            theirs[zz, 2, high] = total.astype(bf16)

        face(zz).start()

    def column(step):
        zz = p.order(step, True)
        side(zz).wait_recv()
        face(zz).wait_recv()
        base = (get(theirs, (zz, 0)), get(side_in, (zz,)), get(face_in, (zz,)))
        if step == line - 1:
            add_rows(0, count, put(out, ()), *base)

            @pl.when(z > 0)
            def _():
                up(zz).wait_recv()
                add_rows(0, count, put(out, ()), get(out, ()), get(up_in, (zz,)))

            @pl.when(z < line - 1)
            def _():
                down(zz).wait_recv()
                add_rows(0, count, put(out, ()), get(out, ()), get(down_in, (zz,)))

            return

        def onward(copy, source, more):
            @pl.when(more)
            def _():
                copy(zz).wait_recv()
                add_rows(0, count, put(theirs, (zz, 0)), *base, get(source, (zz,)))

            @pl.when(jnp.logical_not(more))
            def _():
                add_rows(0, count, put(theirs, (zz, 0)), *base)

            copy(zz).start()

        pl.when(zz > z)(lambda: onward(up, up_in, z > 0))
        pl.when(zz < z)(lambda: onward(down, down_in, z < line - 1))

    for step in range(line + 2):
        if step < line:
            corner(step)
        if 0 <= step - 1 < line:
            plane(step - 1)
        if 0 <= step - 2 < line:
            column(step - 2)
        if job is not None and step < 4:
            job(step, ready, held_in, held_out)
            if step == 3:
                for copy in leaving:
                    copy.start()

    for zz in range(line):
        for flip in range(4):
            core(zz, flip).wait_send()
        for one in (half0, half1, side, face):
            one(zz).wait_send()
        pl.when(zz > z)(lambda zz=zz: up(zz).wait_send())
        pl.when(zz < z)(lambda zz=zz: down(zz).wait_send())
    if job is not None:
        for copy in leaving:
            copy.wait()


def scatter_sum(part, number, job, plain, arrays):
    line = lax.axis_size("dp") // 2
    _, rows, width = part.shape
    results = jax.eval_shape(plain, *arrays)
    size = sum(a.size * a.dtype.itemsize for a in list(arrays) + list(results))
    extra = None
    if size + 13 * line * rows * width * 2 > 52 * 2**20:
        extra, job, arrays, results = plain(*arrays), None, (), ()
    anywhere = pl.BlockSpec(memory_space=pl.ANY)
    more = []
    if job is not None:
        more = [pltpu.VMEM(a.shape, a.dtype) for a in list(arrays) + list(results)] + [
            pltpu.SemaphoreType.DMA((len(arrays),)),
            pltpu.SemaphoreType.DMA((len(results),)),
        ]
    total, *done = pl.pallas_call(
        functools.partial(scatter_kernel, line, job, len(arrays), len(results)),
        out_shape=[jax.ShapeDtypeStruct((rows, width), f32)]
        + [jax.ShapeDtypeStruct(r.shape, r.dtype) for r in results],
        in_specs=[anywhere] * (1 + len(arrays)),
        out_specs=[pl.BlockSpec(memory_space=pltpu.VMEM)] + [anywhere] * len(results),
        scratch_shapes=[
            pltpu.VMEM((line, 4, rows, width), bf16),
            pltpu.VMEM((line, 4, rows, width), bf16),
            pltpu.VMEM((line, 2, rows // 2, width), bf16),
            pltpu.VMEM((line, rows, width), bf16),
            pltpu.VMEM((line, rows, width), bf16),
            pltpu.VMEM((line, rows, width), bf16),
            pltpu.VMEM((line, rows, width), bf16),
            pltpu.SemaphoreType.DMA((10, line)),
            pltpu.SemaphoreType.DMA((10, line)),
            pltpu.SemaphoreType.DMA((4, line)),
        ] + more,
        compiler_params=pltpu.CompilerParams(
            collective_id=number, has_side_effects=True, vmem_limit_bytes=62 * 2**20
        ),
        name=f"scatter{number}",
    )(part, *arrays)
    return total, tuple(done) if extra is None else extra


def last_kernel(line, small, grad, held, rows_out, send, recv, keep, tsend, trecv, tkeep):
    p = Place(line)
    p.greet()
    here = p.y * 2 + p.c
    other = (1 - p.y) * 2 + p.c

    def tremote(src, where, i, device):
        return pltpu.make_async_remote_copy(
            src_ref=src, dst_ref=rows_out.at[where], send_sem=tsend.at[i], recv_sem=trecv.at[i],
            device_id=device, device_id_type=MESH,
        )

    partner = p.device(p.z, 0, 1 - p.c)
    keeping = pltpu.make_async_copy(grad, rows_out.at[here], tkeep)
    keeping.start()
    across = tremote(grad, here, 0, p.device(p.z, 2, p.c))
    beside = tremote(grad, here, 1, partner)
    relay = tremote(rows_out.at[other], other, 2, partner)
    across.start()
    beside.start()
    one = Gather(p, small, held, send, recv, keep)
    for step in range(line + 2):
        one.slot(step)
        if step == 1:
            across.wait_recv()
            relay.start()
    one.finish()
    beside.wait_recv()
    relay.wait_recv()
    for copy in (across, beside, relay):
        copy.wait_send()
    keeping.wait()


def gather_last(small, grad, number):
    line = lax.axis_size("dp") // 2
    devices, quarters = lax.axis_size(AXES), lax.axis_size("tensor")
    anywhere = pl.BlockSpec(memory_space=pl.ANY)
    return pl.pallas_call(
        functools.partial(last_kernel, line),
        out_shape=[
            jax.ShapeDtypeStruct((devices,) + small.shape, small.dtype),
            jax.ShapeDtypeStruct((quarters,) + grad.shape, grad.dtype),
        ],
        in_specs=[pl.BlockSpec(memory_space=pltpu.VMEM)] * 2,
        out_specs=[anywhere, anywhere],
        scratch_shapes=[
            pltpu.SemaphoreType.DMA((10, line)),
            pltpu.SemaphoreType.DMA((10, line)),
            pltpu.SemaphoreType.DMA,
            pltpu.SemaphoreType.DMA((3,)),
            pltpu.SemaphoreType.DMA((3,)),
            pltpu.SemaphoreType.DMA,
        ],
        compiler_params=pltpu.CompilerParams(collective_id=number, has_side_effects=True),
        name=f"last{number}",
    )(small, grad)


def per_device(
    hidden, norm_gain, expert_ids, gate_probs, out_grad, gate_weight, up_weight, down_weight
):
    quarters = lax.axis_size("tensor")
    quarter = lax.axis_index("tensor")
    own_count = hidden.shape[0] // quarters
    width = hidden.shape[1]
    top_count = expert_ids.shape[1]
    devices = lax.axis_size(AXES)
    experts = gate_weight.shape[0] * devices
    capacity = 2 * own_count * top_count // experts
    tokens = own_count * devices
    blocks_in = min(4, devices)
    groups = devices // blocks_in
    gtok = own_count * blocks_in
    gslots = capacity * blocks_in
    slots = groups * gslots
    me = lax.axis_index(AXES)

    own_rows = lax.dynamic_slice_in_dim(hidden, quarter * own_count, own_count, 0)
    values = own_rows.astype(f32)
    inverse = lax.rsqrt(jnp.mean(values * values, axis=-1, keepdims=True) + epsilon)
    unit_rows = values * inverse
    normed = (unit_rows * norm_gain).astype(bf16)
    grad_rows = out_grad.astype(f32)

    meta = jnp.concatenate(
        [
            expert_ids.astype(f32),
            gate_probs,
            jnp.zeros((own_count, 128 - 2 * top_count), f32),
        ],
        axis=1,
    )
    meta_all, normed_all, grads_all = gather_all(
        [meta, normed, out_grad], (0, 0, lax.axis_size("dp") // 2 - 1), 0
    )
    meta_all = meta_all.reshape(tokens, 128)
    ids_all = meta_all[:, :top_count].astype(jnp.int32)
    probs_all = meta_all[:, top_count:2 * top_count]

    hits = ids_all == me
    member = jnp.any(hits, axis=1).reshape(devices, own_count)
    prob = jnp.sum(jnp.where(hits, probs_all, 0.0), axis=1)
    place = jnp.cumsum(member.astype(jnp.int32), axis=1) - 1
    block = jnp.arange(devices, dtype=jnp.int32)[:, None] % blocks_in
    slot = jnp.where(member, block * capacity + place, -1).reshape(groups, gtok)
    picks = slot[:, None, :] == jnp.arange(gslots, dtype=jnp.int32)[None, :, None]
    choose = picks.astype(bf16)
    slot_prob = jnp.sum(
        jnp.where(picks, prob.reshape(groups, 1, gtok), 0.0), axis=2
    ).reshape(slots, 1)

    def pack(rows):
        return jnp.einsum(
            "gst,gtd->gsd", choose, rows.reshape(groups, gtok, width), preferred_element_type=f32
        ).astype(bf16).reshape(slots, width)

    def spread(rows):
        return jnp.einsum(
            "gst,gsd->gtd", choose, rows.reshape(groups, gslots, width), preferred_element_type=f32
        ).astype(bf16).reshape(devices, own_count, width)

    w_gate, w_up, w_down = gate_weight[0], up_weight[0], down_weight[0]
    inputs = pack(normed_all)
    gate_pre = dot(inputs, w_gate, 1, 0)
    up_pre = dot(inputs, w_up, 1, 0)
    sigma = jax.nn.sigmoid(gate_pre)
    silu_vals = gate_pre * sigma
    act = (silu_vals * up_pre).astype(bf16)
    results = dot(act, w_down, 1, 0).astype(bf16)
    results_f = results.astype(f32)
    grads = pack(grads_all).astype(f32)
    cotan = (slot_prob * grads).astype(bf16)
    slot_gg = jnp.sum(grads * results_f, axis=1)
    layer_part, (gate_pgrad, up_pgrad, back) = scatter_sum(
        spread((slot_prob * results_f).astype(bf16)), 1, backward_tile, backward_plain,
        (cotan, gate_pre, up_pre, w_down, w_gate, w_up),
    )
    normed_total, (gate_wgrad, up_wgrad, down_grad) = scatter_sum(
        spread(back), 2, weights_tile, weights_plain,
        (inputs, gate_pgrad, up_pgrad, act, cotan),
    )
    gate_wgrad, up_wgrad, down_grad = gate_wgrad[None], up_wgrad[None], down_grad[None]
    token_gg = jnp.sum(jnp.where(picks, slot_gg.reshape(groups, gslots, 1), 0.0), axis=1)

    layer_out = (values + layer_part).astype(bf16)
    gain_part = jnp.sum(normed_total * unit_rows, axis=0)
    upstream = normed_total * norm_gain
    own_grad = grad_rows + inverse * (
        upstream - unit_rows * jnp.mean(upstream * unit_rows, axis=-1, keepdims=True)
    )
    small = jnp.concatenate([token_gg.reshape(-1, 128), gain_part.reshape(-1, 128)], axis=0)
    small_all, input_grad = gather_last(small, own_grad.astype(bf16), 3)
    input_grad = input_grad.reshape(hidden.shape)
    tiles = tokens // 128
    gain_grad = jnp.sum(small_all[:, tiles:, :], axis=0).reshape(width)
    mine = lax.dynamic_slice_in_dim(
        small_all[:, :tiles, :].reshape(devices, tokens), me * own_count, own_count, 1
    )
    named = expert_ids[:, :, None] == jnp.arange(devices, dtype=jnp.int32)[None, None, :]
    gate_grad = jnp.sum(jnp.where(named, mine.T[:, None, :], 0.0), axis=2)
    return (layer_out, input_grad, gate_grad, gain_grad, gate_wgrad, up_wgrad, down_grad)


def solution(mesh):
    rows, wide = P(AXES, None), P(AXES, None, None)
    in_specs = (P("dp", None), P(), rows, rows, rows, wide, wide, wide)
    out_specs = (rows, P("dp", None), rows, P(), wide, wide, wide)
    return jax.shard_map(
        per_device, mesh=mesh, in_specs=in_specs, out_specs=out_specs, check_vma=False
    )
```
